512 devices in a mesh: ctx: 64 (over x_hi, z, core), head: 8 (over y, x_lo).
Axes of the slice: x: 4 (x_hi: 2, x_lo: 2; x = x_hi * 2 + x_lo), y: 4, z: 16, core: 2. Of those that a mesh axis runs over, the one named last changes fastest.
Arguments:
- queries: bfloat16 [12288, 4096], P('ctx', 'head'), may hold values from -96 to 96
- key_rows: bfloat16 [12288, 4096], P('ctx', 'head'), may hold values from -8 to 8
- value_rows: bfloat16 [12288, 4096], P('ctx', 'head'), may hold values from -6 to 6
- token_rates: float32 [12288, 8], P('ctx', 'head'), may hold values from 0.02 to 1
- fast_one: bfloat16 [8, 512, 512], P('head'), may hold values from -0.25 to 0.25
- fast_three: bfloat16 [8, 512, 512], P('head'), may hold values from -0.25 to 0.25
- fast_two: bfloat16 [8, 512, 512], P('head'), may hold values from -0.25 to 0.25
- head_gain: float32 [8], P('head'), may hold values from 0.5 to 1.5
Outputs:
- window_out: bfloat16 [12288, 4096], P('ctx', 'head')
- fast_out: bfloat16 [12288, 4096], P('ctx', 'head')
The draws below stay inside these ranges and needn't reach their ends.
All inputs are finite; a program needn't handle non-finite values.
Results may differ from the reference program's by a relative error of at most 0.011.
Values may be sent and summed in bfloat16 or wider, within the bound.
No kernel may reach another device: no remote copies, remote signals or barrier semaphores. Data moves between devices by JAX's collectives and lax.ppermute only.
A program may use at most 64 MiB of HBM per device.

```python
import math
import jax
import jax.numpy as jnp
from jax import lax

HEADS = 8
HD = 512
FH = 512
TOK_DEV = 192
WINDOW = 1024
NS_STEPS = 2
TOKENS = 12288
N_CTX = 64


def drawn_pair(key):
    query_base = jnp.clip(jax.random.normal(jax.random.fold_in(key, 11), (TOKENS, HEADS * HD), jnp.float32), -6.0, 6.0)
    key_base = jnp.clip(jax.random.normal(jax.random.fold_in(key, 12), (TOKENS, HEADS * HD), jnp.float32), -6.0, 6.0)
    return (query_base, key_base)


def draw_queries(key, part):
    return drawn_pair(key)[0].astype(jnp.bfloat16)


def draw_key_rows(key, part):
    return drawn_pair(key)[1].astype(jnp.bfloat16)


def steps_of(stream_key, dims, pieces, smallest, top_value):
    def one(dim, blocks):
        steps = jax.random.uniform(jax.random.fold_in(jax.random.fold_in(stream_key, 6), dim), (blocks,), jnp.float32, smallest / len(pieces), top_value / len(pieces))
        return jnp.repeat(jnp.exp(steps), dims[dim] // blocks).reshape((-1,) + (1,) * (len(dims) - dim - 1))

    loudness = one(*pieces[0])
    for cut in pieces[1:]:
        loudness = loudness * one(*cut)
    return loudness


def noise(stream_key, dims, scale, limit, shards=(), kind=jnp.bfloat16):
    array = jax.random.normal(stream_key, dims, jnp.float32) * scale
    if len(shards) > 0:
        array = steps_of(stream_key, dims, shards, -0.22, 0.18) * array
    return jnp.clip(array, min=-limit, max=limit).astype(kind)


def setup_inputs(seed: int = 0) -> dict:
    streams_of = jax.random.split(jax.random.key(seed), 9)
    queries = draw_queries(jax.random.fold_in(streams_of[8], 71), 0)
    key_rows = draw_key_rows(jax.random.fold_in(streams_of[8], 71), 0)
    value_rows = noise(streams_of[2], (TOKENS, HEADS * HD), 1.0, 6.0, ((0, 64), (1, 8)))
    token_rates = jnp.clip(jnp.exp(math.log(1.0) - 3.912023 * jax.random.uniform(streams_of[3], (TOKENS, HEADS), jnp.float32) ** steps_of(streams_of[3], (TOKENS, HEADS), ((0, 64), (1, 8)), -0.2, 0.2)), 0.02, 1.0)
    fast_one = noise(streams_of[4], (HEADS, HD, FH), HD ** -0.5, 0.25, ((0, 8),))
    fast_three = noise(streams_of[5], (HEADS, HD, FH), HD ** -0.5, 0.25, ((0, 8),))
    fast_two = noise(streams_of[6], (HEADS, FH, HD), FH ** -0.5, 0.25, ((0, 8),))
    head_gain = jnp.clip(jnp.exp(math.log(1.5) - 1.0986123 * jax.random.uniform(streams_of[7], (HEADS,), jnp.float32) ** steps_of(streams_of[7], (HEADS,), ((0, 8),), -0.2, 0.2)), 0.5, 1.5)
    return {"queries": queries, "key_rows": key_rows, "value_rows": value_rows, "token_rates": token_rates, "fast_one": fast_one, "fast_three": fast_three, "fast_two": fast_two, "head_gain": head_gain}


COEF_A = 3.4445
COEF_B = -4.775
COEF_C = 2.0315
EPSILON = 1e-06

def rms_rows(block):
    return block / jnp.sqrt(lax.optimization_barrier(jnp.mean(block * block, axis=-1, keepdims=True)) + EPSILON)

def orthogonal(gradient):
    squares = jnp.sum(gradient * gradient)
    current = lax.optimization_barrier((gradient / (jnp.sqrt(squares) + 1e-07)).astype(jnp.bfloat16))
    for sweep_index in range(NS_STEPS):
        gram_matrix = lax.optimization_barrier(jnp.dot(current, current.T, preferred_element_type=jnp.float32).astype(jnp.bfloat16))
        mixer = (COEF_B * gram_matrix.astype(jnp.float32) + COEF_C * jnp.dot(gram_matrix, gram_matrix, preferred_element_type=jnp.float32)).astype(jnp.bfloat16)
        current = lax.optimization_barrier((COEF_A * current.astype(jnp.float32) + jnp.dot(mixer, current, preferred_element_type=jnp.float32)).astype(jnp.bfloat16))
    return current

def fast_head(operands):
    query_block, key_block, value_block, rate_column, weight_one, weight_three, weight_two = operands
    key_normed = rms_rows(key_block.astype(jnp.float32)).astype(jnp.bfloat16)
    query_normed = rms_rows(query_block.astype(jnp.float32)).astype(jnp.bfloat16)
    hidden_one = jnp.dot(key_normed, weight_one, preferred_element_type=jnp.float32)
    hidden_three = jnp.dot(key_normed, weight_three, preferred_element_type=jnp.float32)
    sigmoid_one = jax.nn.sigmoid(hidden_one)
    active = hidden_one * sigmoid_one
    hidden = (active * hidden_three).astype(jnp.bfloat16)
    delta_out = (-rate_column[:, None] * value_block.astype(jnp.float32)).astype(jnp.bfloat16)
    delta_hidden = jnp.dot(delta_out, weight_two.T, preferred_element_type=jnp.float32)
    delta_three = (delta_hidden * active).astype(jnp.bfloat16)
    delta_one = (delta_hidden * hidden_three * sigmoid_one * (1.0 + hidden_one * (1.0 - sigmoid_one))).astype(jnp.bfloat16)
    gradient_one = jnp.dot(key_normed.T, delta_one, preferred_element_type=jnp.float32)
    gradient_three = jnp.dot(key_normed.T, delta_three, preferred_element_type=jnp.float32)
    gradient_two = jnp.dot(hidden.T, delta_out, preferred_element_type=jnp.float32)
    new_one = (weight_one.astype(jnp.float32) - orthogonal(gradient_one).astype(jnp.float32)).astype(jnp.bfloat16)
    new_three = (weight_three.astype(jnp.float32) - orthogonal(gradient_three).astype(jnp.float32)).astype(jnp.bfloat16)
    new_two = (weight_two.astype(jnp.float32) - orthogonal(gradient_two).astype(jnp.float32)).astype(jnp.bfloat16)
    query_one = jnp.dot(query_normed, new_one, preferred_element_type=jnp.float32)
    query_three = jnp.dot(query_normed, new_three, preferred_element_type=jnp.float32)
    query_hidden = (jax.nn.silu(query_one) * query_three).astype(jnp.bfloat16)
    return jnp.dot(query_hidden, new_two, preferred_element_type=jnp.float32)

def window_head(operands):
    query_block, key_block, value_block = operands
    padded_keys = jnp.concatenate([jnp.zeros((WINDOW, HD), jnp.bfloat16), key_block], axis=0)
    padded_values = jnp.concatenate([jnp.zeros((WINDOW, HD), jnp.bfloat16), value_block], axis=0)

    def one_block(block_index):
        start = (block_index * TOK_DEV).astype(jnp.int32)
        queries_here = lax.dynamic_slice_in_dim(query_block, start, TOK_DEV, 0)
        keys_here = lax.dynamic_slice_in_dim(padded_keys, start, TOK_DEV + WINDOW, 0)
        values_here = lax.dynamic_slice_in_dim(padded_values, start, TOK_DEV + WINDOW, 0)
        scores = jnp.dot(queries_here, keys_here.T, preferred_element_type=jnp.float32) * HD ** (-0.5)
        query_pos = lax.broadcasted_iota(jnp.int32, (TOK_DEV, TOK_DEV + WINDOW), 0) + WINDOW
        key_pos = lax.broadcasted_iota(jnp.int32, (TOK_DEV, TOK_DEV + WINDOW), 1)
        offset = query_pos - key_pos
        allowed = (offset >= 0) & (offset < WINDOW) & (key_pos + start - WINDOW >= 0)
        scores = jnp.where(allowed, scores, -1e+30)
        row_top = lax.optimization_barrier(jnp.max(scores, axis=-1, keepdims=True))
        exponent = jnp.exp(scores - row_top)
        weights = (exponent / lax.optimization_barrier(jnp.sum(exponent, axis=-1, keepdims=True))).astype(jnp.bfloat16)
        return jnp.dot(weights, values_here, preferred_element_type=jnp.float32)
    blocks = lax.map(one_block, jnp.arange(N_CTX, dtype=jnp.int32))
    return blocks.reshape(TOKENS, HD)

def reference(queries, key_rows, value_rows, token_rates, fast_one, fast_three, fast_two, head_gain):
    split_q = queries.reshape(TOKENS, HEADS, HD).transpose(1, 0, 2)
    split_k = key_rows.reshape(TOKENS, HEADS, HD).transpose(1, 0, 2)
    split_v = value_rows.reshape(TOKENS, HEADS, HD).transpose(1, 0, 2)
    attended = lax.map(window_head, (split_q, split_k, split_v)).transpose(1, 0, 2)
    fast = lax.map(fast_head, (split_q, split_k, split_v, token_rates.T, fast_one, fast_three, fast_two))
    fast = (fast * head_gain[:, None, None]).transpose(1, 0, 2)
    window_out = attended / jnp.sqrt(lax.optimization_barrier(jnp.mean(attended * attended, axis=(1, 2), keepdims=True)) + EPSILON)
    fast_out = fast / jnp.sqrt(lax.optimization_barrier(jnp.mean(fast * fast, axis=(1, 2), keepdims=True)) + EPSILON)
    return (window_out.reshape(TOKENS, HEADS * HD).astype(jnp.bfloat16), fast_out.reshape(TOKENS, HEADS * HD).astype(jnp.bfloat16))
```

```python
import functools

import jax
import jax.numpy as jnp
from jax import lax
from jax.experimental import pallas as pl
from jax.experimental.pallas import tpu as pltpu
from jax.sharding import Mesh
from jax.sharding import PartitionSpec as P

HEADS = 8
HD = 512
FH = 512
WINDOW = 1024
NS_STEPS = 2
TOK = 192
PART = 128
ROWS = 3 * PART

COEF_A = 3.4445
COEF_B = -4.775
COEF_C = 2.0315
EPSILON = 1e-06

CHIPS = ("xh", "zh", "zl")
RING = ("zh", "zl")
SAME = ("xh", "zh")

NT = (((1,), (1,)), ((), ()))
TN = (((0,), (0,)), ((), ()))


def shifted(x, axes, by):
    count = lax.axis_size(axes)
    return lax.ppermute(x, axes, [(i, (i + by) % count) for i in range(count)])


def nt(a, b):
    return lax.dot_general(a, b, NT, preferred_element_type=jnp.float32)


def nn(a, b):
    return jnp.dot(a, b, preferred_element_type=jnp.float32)


def sigmoid(x):
    return 1.0 / (1.0 + jnp.exp(-x))


def grad_kernel(first, ids_ref, pa_ref, pb_ref, w1_ref, w3_ref, w2_ref, *rest):
    if first:
        (out_ref,) = rest
    else:
        sofar_ref, out_ref = rest
    w13 = jnp.concatenate([w1_ref[...], w3_ref[...]], axis=0)
    w2 = w2_ref[...]
    ones = jnp.ones((8, HD), jnp.bfloat16)
    g13 = None
    g2 = None
    for ref in (pa_ref, pb_ref):
        k = ref[0:TOK, :]
        v = ref[TOK : 2 * TOK, :]
        extra = ref[2 * TOK : 2 * TOK + 16, :].astype(jnp.float32)
        rate = -(extra[0:1, 0:TOK] + extra[1:2, 0:TOK])
        kf = k.astype(jnp.float32)
        squares = nt(ones, (kf * kf).astype(jnp.bfloat16))
        scale = lax.rsqrt(squares[0:1, :] * (1.0 / HD) + EPSILON)
        both = nt(w13, k) * scale
        a = both[:PART]
        b = both[PART:]
        s = sigmoid(a)
        u = a * s
        dh = nt(w2, v) * rate
        hid = (u * b * rate).astype(jnp.bfloat16)
        d1 = (dh * b * s * (1.0 + a * (1.0 - s)) * scale).astype(jnp.bfloat16)
        d3 = (dh * u * scale).astype(jnp.bfloat16)
        p13 = nn(jnp.concatenate([d1, d3], axis=0), k)
        p2 = nn(hid, v)
        g13 = p13 if g13 is None else g13 + p13
        g2 = p2 if g2 is None else g2 + p2
    if first:
        out_ref[0 : 2 * PART, :] = g13
        out_ref[2 * PART : ROWS, :] = g2
    else:
        out_ref[0 : 2 * PART, :] = (g13 + sofar_ref[0 : 2 * PART, :]).astype(jnp.bfloat16)
        out_ref[2 * PART : ROWS, :] = (g2 + sofar_ref[2 * PART : ROWS, :]).astype(jnp.bfloat16)


def gradients(first, ids, pa, pb, w1t, w3t, w2, sofar=None):
    whole = lambda a: pl.BlockSpec(a.shape, lambda i, ids: (0,) * a.ndim)
    mine = pl.BlockSpec((PART, HD), lambda i, ids: (ids[0], 0))
    args = [pa, pb, w1t, w3t, w2]
    specs = [whole(pa), whole(pb), mine, mine, mine]
    if not first:
        args.append(sofar)
        specs.append(whole(sofar))
    return pl.pallas_call(
        functools.partial(grad_kernel, first),
        out_shape=jax.ShapeDtypeStruct((ROWS, HD), jnp.float32 if first else jnp.bfloat16),
        grid_spec=pltpu.PrefetchScalarGridSpec(
            num_scalar_prefetch=1,
            grid=(1,),
            in_specs=specs,
            out_specs=pl.BlockSpec((ROWS, HD), lambda i, ids: (0, 0)),
        ),
        name="grad_first" if first else "grad_second",
    )(ids, *args)


def solve_kernel(ids_ref, gain_ref, q_ref, w1_ref, w3_ref, w2_ref, ga, gb, gc, gd, o_ref, sq_ref):
    slots = (ga, gb, gc, gd)
    fresh = []
    for m, w_ref in enumerate((w1_ref, w3_ref, w2_ref)):
        g = jnp.concatenate([r[m * PART : (m + 1) * PART, :] for r in slots], axis=0).astype(
            jnp.float32
        )
        norm = jnp.sqrt(jnp.sum(g * g, keepdims=True)) + 1e-07
        x = (g / norm).astype(jnp.bfloat16)
        for _ in range(NS_STEPS):
            gram = nt(x, x).astype(jnp.bfloat16)
            mixer = (COEF_B * gram.astype(jnp.float32) + COEF_C * nn(gram, gram)).astype(
                jnp.bfloat16
            )
            x = (COEF_A * x.astype(jnp.float32) + nn(mixer, x)).astype(jnp.bfloat16)
        w = jnp.concatenate(
            [w_ref[pl.ds(pl.multiple_of(ids_ref[i] * PART, PART), PART), :] for i in range(4)],
            axis=0,
        )
        fresh.append((w.astype(jnp.float32) - x.astype(jnp.float32)).astype(jnp.bfloat16))
    q = q_ref[...].astype(jnp.float32)
    qn = (q * lax.rsqrt(jnp.mean(q * q, axis=-1, keepdims=True) + EPSILON)).astype(jnp.bfloat16)
    h1 = nt(qn, fresh[0])
    h3 = nt(qn, fresh[1])
    hidden = (h1 * sigmoid(h1) * h3).astype(jnp.bfloat16)
    o = nn(hidden, fresh[2]) * gain_ref[0]
    o_ref[...] = o
    sq_ref[...] = lax.dot_general(
        jnp.ones((8, HD), jnp.float32), o * o, NT,
        precision=lax.Precision.HIGHEST, preferred_element_type=jnp.float32,
    )


def solve(ids, gain, q, w1t, w3t, w2, slots):
    vmem = pl.BlockSpec(memory_space=pltpu.VMEM)
    smem = pl.BlockSpec(memory_space=pltpu.SMEM)
    return pl.pallas_call(
        solve_kernel,
        out_shape=(
            jax.ShapeDtypeStruct((TOK, HD), jnp.float32),
            jax.ShapeDtypeStruct((8, TOK), jnp.float32),
        ),
        in_specs=[smem, smem] + [vmem] * 8,
        out_specs=(vmem, vmem),
        name="solve",
    )(ids, gain, q, w1t, w3t, w2, *slots)


def window_kernel(info_ref, q_ref, *refs):
    blocks = refs[:8]
    o_ref, sq_ref = refs[8:]
    core = info_ref[0]
    start = info_ref[1]
    places = (
        0, 1 - 2 * core, -2, -1 - 2 * core, -4, -3 - 2 * core, -6, -5 - 2 * core
    )
    q = q_ref[...]
    row = lax.broadcasted_iota(jnp.int32, (TOK, TOK), 0)
    col = lax.broadcasted_iota(jnp.int32, (TOK, TOK), 1)
    scores = []
    for ref, place in zip(blocks, places):
        s = nt(q, ref[0:TOK, :]) * HD ** (-0.5)
        offset = row - col - place * TOK
        allowed = (offset >= 0) & (offset < WINDOW) & (col + (start + place) * TOK >= 0)
        scores.append(jnp.where(allowed, s, -1e30))
    top = functools.reduce(jnp.maximum, scores)
    top = jnp.max(top, axis=-1, keepdims=True)
    weights = [jnp.exp(s - top) for s in scores]
    total = jnp.sum(functools.reduce(jnp.add, weights), axis=-1, keepdims=True)
    inverse = 1.0 / total
    o = None
    for ref, w in zip(blocks, weights):
        part = nn((w * inverse).astype(jnp.bfloat16), ref[TOK : 2 * TOK, :])
        o = part if o is None else o + part
    o_ref[...] = o
    sq_ref[...] = lax.dot_general(
        jnp.ones((8, HD), jnp.float32), o * o, NT,
        precision=lax.Precision.HIGHEST, preferred_element_type=jnp.float32,
    )


def window_attention(info, q, blocks):
    vmem = pl.BlockSpec(memory_space=pltpu.VMEM)
    smem = pl.BlockSpec(memory_space=pltpu.SMEM)
    return pl.pallas_call(
        window_kernel,
        out_shape=(
            jax.ShapeDtypeStruct((TOK, HD), jnp.float32),
            jax.ShapeDtypeStruct((8, TOK), jnp.float32),
        ),
        in_specs=[smem] + [vmem] * 9,
        out_specs=(vmem, vmem),
        name="window",
    )(info, q, *blocks)


def finish_kernel(sums_ref, a_ref, o_ref, wo_ref, fo_ref):
    ones = jnp.ones((HEADS, 128), jnp.float32)
    for which, (src, dst) in enumerate(((a_ref, wo_ref), (o_ref, fo_ref))):
        total = lax.dot_general(
            sums_ref[:, which, :], ones, TN,
            precision=lax.Precision.HIGHEST, preferred_element_type=jnp.float32,
        )[:, 0:1]
        dst[...] = (src[...] * lax.rsqrt(total * (1.0 / (HEADS * HD)) + EPSILON)).astype(
            jnp.bfloat16
        )


def finish(sums, attended, fast):
    vmem = pl.BlockSpec(memory_space=pltpu.VMEM)
    return pl.pallas_call(
        finish_kernel,
        out_shape=(
            jax.ShapeDtypeStruct((TOK, HD), jnp.bfloat16),
            jax.ShapeDtypeStruct((TOK, HD), jnp.bfloat16),
        ),
        in_specs=[vmem] * 3,
        out_specs=(vmem, vmem),
        name="finish",
    )(sums, attended, fast)


def local(queries, key_rows, value_rows, token_rates, fast_one, fast_three, fast_two, head_gain):
    zl = lax.axis_index("zl")
    core = lax.axis_index("core")
    chip = lax.axis_index(CHIPS)
    ids = jnp.stack(
        [zl * 2 + core, zl * 2 + 1 - core, (1 - zl) * 2 + core, (1 - zl) * 2 + 1 - core]
    ).astype(jnp.int32)
    info = jnp.stack([core, chip * 2 + core]).astype(jnp.int32)

    rate = token_rates[:, 0]
    high = lax.reduce_precision(rate, 8, 7)
    extra = jnp.stack([high, rate - high]).astype(jnp.bfloat16)
    extra = jnp.pad(extra, ((0, 14), (0, HD - TOK)))
    own = jnp.concatenate([key_rows, value_rows, extra], axis=0)

    back1 = shifted(own, CHIPS, 1)
    own_x = shifted(own, "core", 1)
    w1t = fast_one[0].T
    w3t = fast_three[0].T
    w2 = fast_two[0]
    sofar = gradients(True, ids, own, own_x, w1t, w3t, w2)
    back1_x = shifted(back1, "core", 1)
    back2 = shifted(back1[: 2 * TOK], CHIPS, 1)
    partial = gradients(False, ids, back1, back1_x, w1t, w3t, w2, sofar)

    pieces = lax.all_to_all(partial.reshape(16, ROWS // 16, HD), SAME, 0, 0)
    piece = jnp.sum(pieces.astype(jnp.float32), axis=0).astype(jnp.bfloat16)

    back2_x = shifted(back2, "core", 1)
    back3 = shifted(back2, CHIPS, 1)
    back3_x = shifted(back3, "core", 1)
    attended, attended_sq = window_attention(
        info, queries, (own, own_x, back1, back1_x, back2, back2_x, back3, back3_x)
    )

    spread = jnp.broadcast_to(piece[None], (16,) + piece.shape)
    mine = lax.all_to_all(spread, SAME, 0, 0).reshape(ROWS, HD)
    mine_x = shifted(mine, "core", 1)
    upper = shifted(mine[ROWS // 2 :], RING, 1)
    lower = shifted(mine[: ROWS // 2], RING, -1)
    other = jnp.concatenate([lower, upper], axis=0)
    other_x = shifted(other, "core", 1)

    fast, fast_sq = solve(
        ids, head_gain, queries, w1t, w3t, w2, (mine, mine_x, other, other_x)
    )
    sums = jnp.concatenate([attended_sq[0:1], fast_sq[0:1]], axis=0)
    sums = lax.all_to_all(jnp.broadcast_to(sums[None], (HEADS,) + sums.shape), "head", 0, 0)
    return finish(sums, attended, fast)


def solution(mesh):
    fine = Mesh(mesh.devices.reshape(2, 8, 2, 2, 8), ("xh", "zh", "zl", "core", "head"))
    ctx = ("xh", "zh", "zl", "core")
    return jax.shard_map(
        local,
        mesh=fine,
        in_specs=(
            P(ctx, "head"),
            P(ctx, "head"),
            P(ctx, "head"),
            P(ctx, "head"),
            P("head", None, None),
            P("head", None, None),
            P("head", None, None),
            P("head"),
        ),
        out_specs=(P(ctx, "head"), P(ctx, "head")),
        check_vma=False,
    )
```

```python
import functools

import jax
import jax.numpy as jnp
from jax import lax
from jax.experimental import pallas as pl
from jax.experimental.pallas import tpu as pltpu
from jax.sharding import Mesh
from jax.sharding import PartitionSpec as P

HEADS = 8
HD = 512
WINDOW = 1024
NS_STEPS = 2
TOK = 192
PART = 128
ROWS = 3 * PART

COEF_A = 3.4445
COEF_B = -4.775
COEF_C = 2.0315
EPSILON = 1e-06

HALF = ROWS // 2
FAR = 128

CHIPS = ("xh", "zq", "zm", "zl")
RING = ("zq", "zm", "zl")
SAME = ("zm", "xh", "zq")
KIN = ("xh", "zq")

NT = (((1,), (1,)), ((), ()))
TN = (((0,), (0,)), ((), ()))


def shifted(x, axes, by):
    count = lax.axis_size(axes)
    return lax.ppermute(x, axes, [(i, (i + by) % count) for i in range(count)])


def exchanged(x, axes):
    return lax.all_to_all(x, axes, 0, 0)


def nt(a, b):
    return lax.dot_general(a, b, NT, preferred_element_type=jnp.float32)


def nn(a, b):
    return jnp.dot(a, b, preferred_element_type=jnp.float32)


def near(x):
    return pltpu.with_memory_space_constraint(x, pltpu.MemorySpace.VMEM)


def near_out(shape, dtype):
    return pltpu.MemorySpace.VMEM(shape, dtype)


def sigmoid(x):
    return 1.0 / (1.0 + jnp.exp(-x))


def grad_kernel(first, ids_ref, pa_ref, pb_ref, w1_ref, w3_ref, w2_ref, *rest):
    if first:
        (out_ref,) = rest
    else:
        sofar_ref, out_ref = rest
    mine = pl.ds(pl.multiple_of(ids_ref[0] * PART, PART), PART)
    w13 = jnp.concatenate([w1_ref[mine, :], w3_ref[mine, :]], axis=0)
    w2 = w2_ref[mine, :]
    ones = jnp.ones((8, HD), jnp.bfloat16)
    g13 = None
    g2 = None
    for ref in (pa_ref, pb_ref):
        k = ref[0:TOK, :]
        v = ref[TOK : 2 * TOK, :]
        extra = ref[2 * TOK : 2 * TOK + 16, :].astype(jnp.float32)
        rate = -(extra[0:1, 0:TOK] + extra[1:2, 0:TOK])
        kf = k.astype(jnp.float32)
        squares = nt(ones, (kf * kf).astype(jnp.bfloat16))
        scale = lax.rsqrt(squares[0:1, :] * (1.0 / HD) + EPSILON)
        both = nt(w13, k) * scale
        a = both[:PART]
        b = both[PART:]
        s = sigmoid(a)
        u = a * s
        dh = nt(w2, v) * rate
        hid = (u * b * rate).astype(jnp.bfloat16)
        d1 = (dh * b * s * (1.0 + a * (1.0 - s)) * scale).astype(jnp.bfloat16)
        d3 = (dh * u * scale).astype(jnp.bfloat16)
        p13 = nn(jnp.concatenate([d1, d3], axis=0), k)
        p2 = nn(hid, v)
        g13 = p13 if g13 is None else g13 + p13
        g2 = p2 if g2 is None else g2 + p2
    if first:
        out_ref[0 : 2 * PART, :] = g13
        out_ref[2 * PART : ROWS, :] = g2
    else:
        out_ref[0 : 2 * PART, :] = (g13 + sofar_ref[0 : 2 * PART, :]).astype(jnp.bfloat16)
        out_ref[2 * PART : ROWS, :] = (g2 + sofar_ref[2 * PART : ROWS, :]).astype(jnp.bfloat16)


VMEM = pl.BlockSpec(memory_space=pltpu.VMEM)
SMEM = pl.BlockSpec(memory_space=pltpu.SMEM)


def gradients(first, ids, *arrays):
    return pl.pallas_call(
        functools.partial(grad_kernel, first),
        out_shape=near_out((ROWS, HD), jnp.float32)
        if first
        else jax.ShapeDtypeStruct((ROWS, HD), jnp.bfloat16),
        in_specs=[SMEM] + [VMEM] * len(arrays),
        out_specs=VMEM,
        compiler_params=pltpu.CompilerParams(vmem_limit_bytes=16 << 20),
        name="grad_first" if first else "grad_second",
    )(ids, *[near(x) for x in arrays])


def solve_kernel(ids_ref, gain_ref, q_ref, w1_ref, w3_ref, w2_ref, g_ref, gx_ref, o_ref, sq_ref):
    low = ids_ref[4] == 0
    near_low = ids_ref[4] == ids_ref[5]
    slots = []
    for first, second, when in ((0, HALF, low), (3 * HALF, 2 * HALF, near_low)):
        for ref in (g_ref, gx_ref):
            a = ref[first : first + HALF, :]
            b = ref[second : second + HALF, :]
            slots.append(
                jnp.concatenate([jnp.where(when, a, b), jnp.where(when, b, a)], axis=0)
            )
    fresh = []
    for m, w_ref in enumerate((w1_ref, w3_ref, w2_ref)):
        g = jnp.concatenate([r[m * PART : (m + 1) * PART, :] for r in slots], axis=0).astype(
            jnp.float32
        )
        norm = jnp.sqrt(jnp.sum(g * g, keepdims=True)) + 1e-07
        x = (g / norm).astype(jnp.bfloat16)
        for _ in range(NS_STEPS):
            gram = nt(x, x).astype(jnp.bfloat16)
            mixer = (COEF_B * gram.astype(jnp.float32) + COEF_C * nn(gram, gram)).astype(
                jnp.bfloat16
            )
            x = (COEF_A * x.astype(jnp.float32) + nn(mixer, x)).astype(jnp.bfloat16)
        w = jnp.concatenate(
            [w_ref[pl.ds(pl.multiple_of(ids_ref[i] * PART, PART), PART), :] for i in range(4)],
            axis=0,
        )
        fresh.append((w.astype(jnp.float32) - x.astype(jnp.float32)).astype(jnp.bfloat16))
    q = q_ref[...].astype(jnp.float32)
    qn = (q * lax.rsqrt(jnp.mean(q * q, axis=-1, keepdims=True) + EPSILON)).astype(jnp.bfloat16)
    h1 = nt(qn, fresh[0])
    h3 = nt(qn, fresh[1])
    hidden = (h1 * sigmoid(h1) * h3).astype(jnp.bfloat16)
    o = nn(hidden, fresh[2]) * gain_ref[0]
    o_ref[...] = o
    sq_ref[...] = lax.dot_general(
        jnp.ones((8, HD), jnp.float32), o * o, NT,
        precision=lax.Precision.HIGHEST, preferred_element_type=jnp.float32,
    )


def solve(ids, gain, *arrays):
    return pl.pallas_call(
        solve_kernel,
        out_shape=(near_out((TOK, HD), jnp.float32), near_out((8, TOK), jnp.float32)),
        in_specs=[SMEM, SMEM] + [VMEM] * len(arrays),
        out_specs=(VMEM, VMEM),
        compiler_params=pltpu.CompilerParams(vmem_limit_bytes=28 << 20),
        name="solve",
    )(ids, gain, *[near(x) for x in arrays])


def window_kernel(info_ref, q_ref, *refs):
    blocks = refs[:8]
    o_ref, sq_ref = refs[8:]
    core = info_ref[0]
    start = info_ref[1]
    places = (
        (TOK, 0),
        (TOK, TOK * (1 - 2 * core)),
        (TOK, -2 * TOK),
        (TOK, -TOK * (1 + 2 * core)),
        (TOK, -4 * TOK),
        (TOK, -TOK * (3 + 2 * core)),
        (FAR, -WINDOW + (FAR - TOK) * core),
        (FAR, -WINDOW + FAR - (FAR + TOK) * core),
    )
    q = q_ref[...]
    scores = []
    top = None
    for ref, (count, place) in zip(blocks, places):
        row = lax.broadcasted_iota(jnp.int32, (TOK, count), 0)
        col = lax.broadcasted_iota(jnp.int32, (TOK, count), 1)
        s = nt(q, ref[0:count, :]) * HD ** (-0.5)
        offset = row - col - place
        allowed = (offset >= 0) & (offset < WINDOW) & (col + (start * TOK + place) >= 0)
        s = jnp.where(allowed, s, -1e30)
        scores.append(s)
        here = jnp.max(s, axis=-1, keepdims=True)
        top = here if top is None else jnp.maximum(top, here)
    weights = [jnp.exp(s - top) for s in scores]
    total = functools.reduce(jnp.add, [jnp.sum(w, axis=-1, keepdims=True) for w in weights])
    inverse = 1.0 / total
    o = None
    for ref, w, (count, _) in zip(blocks, weights, places):
        part = nn((w * inverse).astype(jnp.bfloat16), ref[count : 2 * count, :])
        o = part if o is None else o + part
    o_ref[...] = o
    sq_ref[...] = lax.dot_general(
        jnp.ones((8, HD), jnp.float32), o * o, NT,
        precision=lax.Precision.HIGHEST, preferred_element_type=jnp.float32,
    )


def window_attention(info, *arrays):
    return pl.pallas_call(
        window_kernel,
        out_shape=(near_out((TOK, HD), jnp.float32), near_out((8, TOK), jnp.float32)),
        in_specs=[SMEM] + [VMEM] * len(arrays),
        out_specs=(VMEM, VMEM),
        compiler_params=pltpu.CompilerParams(vmem_limit_bytes=24 << 20),
        name="window",
    )(info, *[near(x) for x in arrays])


def finish_kernel(sums_ref, a_ref, o_ref, wo_ref, fo_ref):
    ones = jnp.ones((HEADS, 128), jnp.float32)
    for which, (src, dst) in enumerate(((a_ref, wo_ref), (o_ref, fo_ref))):
        total = lax.dot_general(
            sums_ref[:, which, :], ones, TN,
            precision=lax.Precision.HIGHEST, preferred_element_type=jnp.float32,
        )[:, 0:1]
        dst[...] = (src[...] * lax.rsqrt(total * (1.0 / (HEADS * HD)) + EPSILON)).astype(
            jnp.bfloat16
        )


def finish(*arrays):
    return pl.pallas_call(
        finish_kernel,
        out_shape=(
            jax.ShapeDtypeStruct((TOK, HD), jnp.bfloat16),
            jax.ShapeDtypeStruct((TOK, HD), jnp.bfloat16),
        ),
        in_specs=[VMEM] * 3,
        out_specs=(VMEM, VMEM),
        compiler_params=pltpu.CompilerParams(vmem_limit_bytes=8 << 20),
        name="finish",
    )(*[near(x) for x in arrays])


def local(queries, key_rows, value_rows, token_rates, fast_one, fast_three, fast_two, head_gain):
    zl = lax.axis_index("zl")
    zm = lax.axis_index("zm")
    core = lax.axis_index("core")
    chip = lax.axis_index(CHIPS)
    ids = jnp.stack(
        [zl * 2 + core, zl * 2 + 1 - core, 2 - 2 * zl + core, 3 - 2 * zl - core, zm, zl]
    ).astype(jnp.int32)
    info = jnp.stack([core, chip * 2 + core]).astype(jnp.int32)

    rate = token_rates[:, 0]
    high = lax.reduce_precision(rate, 8, 7)
    extra = jnp.stack([high, rate - high]).astype(jnp.bfloat16)
    extra = jnp.pad(extra, ((0, 14), (0, HD - TOK)))
    own = jnp.concatenate([key_rows, value_rows, extra], axis=0)

    back1 = shifted(own, CHIPS, 1)
    own_x = shifted(own, "core", 1)
    w1t = fast_one[0].T
    w3t = fast_three[0].T
    w2 = fast_two[0]
    sofar = gradients(True, ids, own, own_x, w1t, w3t, w2)
    back1, sofar = lax.optimization_barrier((back1, sofar))

    back1_x = shifted(back1, "core", 1)
    back2 = shifted(back1, CHIPS, 1)
    partial = gradients(False, ids, back1, back1_x, w1t, w3t, w2, sofar)
    pieces = exchanged(partial.reshape(16, ROWS // 16, HD), SAME)
    back2_x = shifted(back2, "core", 1)
    cut = TOK - FAR
    far = jnp.where(
        core == 0,
        jnp.concatenate(
            [back2[FAR:TOK], back2_x[:cut], back2[TOK + FAR : 2 * TOK], back2_x[TOK : TOK + cut]]
        ),
        jnp.concatenate([back2[cut:TOK], back2[TOK + cut : 2 * TOK]]),
    )
    back3 = shifted(far, CHIPS, 1)
    back3_x = shifted(back3, "core", 1)
    piece = jnp.sum(pieces.astype(jnp.float32), axis=0).astype(jnp.bfloat16)
    spread = jnp.broadcast_to(piece[None], (8,) + piece.shape)
    mine = exchanged(spread, KIN).reshape(HALF, HD)
    attended, attended_sq = window_attention(
        info, queries, own, own_x, back1, back1_x, back2, back2_x, back3, back3_x
    )
    mine, attended, attended_sq = lax.optimization_barrier((mine, attended, attended_sq))

    up = shifted(mine, RING, 1)
    down = shifted(mine, RING, -1)
    far_up = shifted(mine[HALF // 2 :], RING, 2)
    far_down = shifted(mine[: HALF // 2], RING, -2)
    held = jnp.concatenate([mine, far_down, far_up, up, down], axis=0)
    held_x = shifted(held, "core", 1)

    fast, fast_sq = solve(ids, head_gain, queries, w1t, w3t, w2, held, held_x)
    sums = jnp.concatenate([attended_sq[0:1], fast_sq[0:1]], axis=0)
    sums = exchanged(jnp.broadcast_to(sums[None], (HEADS,) + sums.shape), "head")
    return finish(sums, attended, fast)


def solution(mesh):
    fine = Mesh(mesh.devices.reshape(2, 4, 2, 2, 2, 8), CHIPS + ("core", "head"))
    ctx = CHIPS + ("core",)
    return jax.shard_map(
        local,
        mesh=fine,
        in_specs=(
            P(ctx, "head"),
            P(ctx, "head"),
            P(ctx, "head"),
            P(ctx, "head"),
            P("head", None, None),
            P("head", None, None),
            P("head", None, None),
            P("head"),
        ),
        out_specs=(P(ctx, "head"), P(ctx, "head")),
        check_vma=False,
    )
```

```python
import functools

import jax
import jax.numpy as jnp
from jax import lax
from jax.experimental import pallas as pl
from jax.experimental.pallas import tpu as pltpu
from jax.sharding import Mesh
from jax.sharding import PartitionSpec as P

HEADS = 8
HD = 512
WINDOW = 1024
NS_STEPS = 2
TOK = 192
PART = 128
ROWS = 3 * PART

COEF_A = 3.4445
COEF_B = -4.775
COEF_C = 2.0315
EPSILON = 1e-06

BIT = ROWS // 4
FAR = 128
SPAN = 3

CHIPS = ("xh", "zq", "zm", "zl")
RING = ("zq", "zm", "zl")
SAME = ("zm", "zl", "zq")
KIN = ("xh", "zq")

NT = (((1,), (1,)), ((), ()))
TN = (((0,), (0,)), ((), ()))


def swapped(x, axis):
    return lax.ppermute(x, axis, [(0, 1), (1, 0)])


def forwarded(x):
    count = lax.axis_size(RING)
    return lax.ppermute(x, RING, [(i, (i + 1) % count) for i in range(count)])


def around(x, by):
    count = lax.axis_size(RING)
    pairs = []
    for i in range(count):
        pairs.append((2 * i, 2 * ((i - by) % count)))
        pairs.append((2 * i + 1, 2 * ((i + by) % count) + 1))
    return lax.ppermute(x, RING + ("core",), pairs)


def exchanged(x, axes):
    return lax.all_to_all(x, axes, 0, 0)


def nt(a, b):
    return lax.dot_general(a, b, NT, preferred_element_type=jnp.float32)


def nn(a, b):
    return jnp.dot(a, b, preferred_element_type=jnp.float32)


def near(x):
    return pltpu.with_memory_space_constraint(x, pltpu.MemorySpace.VMEM)


def near_out(shape, dtype):
    return pltpu.MemorySpace.VMEM(shape, dtype)


def sigmoid(x):
    return 1.0 / (1.0 + jnp.exp(-x))


VMEM = pl.BlockSpec(memory_space=pltpu.VMEM)
SMEM = pl.BlockSpec(memory_space=pltpu.SMEM)


def in_lanes(dtype, *columns):
    lane = lax.broadcasted_iota(jnp.int32, (TOK, 128), 1)
    out = jnp.zeros((TOK, 128), jnp.float32)
    for i, column in enumerate(columns):
        out = jnp.where(lane == i, column, out)
    return out.astype(dtype)


def tally_kernel(pieces_ref, out_ref):
    total = jnp.sum(pieces_ref[...].astype(jnp.float32), axis=0).astype(jnp.bfloat16)
    for i in range(out_ref.shape[0]):
        out_ref[i] = total


def tally(pieces, copies):
    return pl.pallas_call(
        tally_kernel,
        out_shape=jax.ShapeDtypeStruct((copies,) + pieces.shape[1:], jnp.bfloat16),
        in_specs=[VMEM],
        out_specs=VMEM,
        compiler_params=pltpu.CompilerParams(vmem_limit_bytes=8 << 20),
        name="tally",
    )(pieces)


def grad_kernel(first, ids_ref, pa_ref, pb_ref, w1_ref, w3_ref, w2_ref, *rest):
    if first:
        (out_ref,) = rest
    else:
        sofar_ref, out_ref = rest
    mine = pl.ds(pl.multiple_of(ids_ref[0] * PART, PART), PART)
    w13 = jnp.concatenate([w1_ref[mine, :], w3_ref[mine, :]], axis=0)
    w2 = w2_ref[mine, :]
    ones = jnp.ones((8, HD), jnp.bfloat16)
    g13 = None
    g2 = None
    for ref in (pa_ref, pb_ref):
        k = ref[0:TOK, :]
        v = ref[TOK : 2 * TOK, :]
        extra = ref[2 * TOK : 2 * TOK + 16, :].astype(jnp.float32)
        rate = -(extra[0:1, 0:TOK] + extra[1:2, 0:TOK])
        kf = k.astype(jnp.float32)
        squares = nt(ones, (kf * kf).astype(jnp.bfloat16))
        scale = lax.rsqrt(squares[0:1, :] * (1.0 / HD) + EPSILON)
        both = nt(w13, k) * scale
        a = both[:PART]
        b = both[PART:]
        s = sigmoid(a)
        u = a * s
        dh = nt(w2, v) * rate
        hid = (u * b * rate).astype(jnp.bfloat16)
        d1 = (dh * b * s * (1.0 + a * (1.0 - s)) * scale).astype(jnp.bfloat16)
        d3 = (dh * u * scale).astype(jnp.bfloat16)
        p13 = nn(jnp.concatenate([d1, d3], axis=0), k)
        p2 = nn(hid, v)
        g13 = p13 if g13 is None else g13 + p13
        g2 = p2 if g2 is None else g2 + p2
    if first:
        out_ref[0 : 2 * PART, :] = g13
        out_ref[2 * PART : ROWS, :] = g2
    else:
        out_ref[0 : 2 * PART, :] = (g13 + sofar_ref[0 : 2 * PART, :]).astype(jnp.bfloat16)
        out_ref[2 * PART : ROWS, :] = (g2 + sofar_ref[2 * PART : ROWS, :]).astype(jnp.bfloat16)


def gradients(first, ids, *arrays):
    return pl.pallas_call(
        functools.partial(grad_kernel, first),
        out_shape=near_out((ROWS, HD), jnp.float32)
        if first
        else jax.ShapeDtypeStruct((ROWS, HD), jnp.bfloat16),
        in_specs=[SMEM] + [VMEM] * len(arrays),
        out_specs=VMEM,
        compiler_params=pltpu.CompilerParams(vmem_limit_bytes=16 << 20),
        name="grad_first" if first else "grad_second",
    )(ids, *[near(x) for x in arrays])


def solve_kernel(
    ids_ref, gain_ref, q_ref, w1_ref, w3_ref, w2_ref, h_ref, hx_ref, a_ref, ax_ref, o_ref, sq_ref, all_ref
):
    core = ids_ref[1]
    place = ids_ref[2]

    def put(ref, row, which, plane, turn):
        start = (plane * 2 + which) * ROWS + lax.rem(place + turn, 4) * BIT
        all_ref[pl.ds(pl.multiple_of(start, 32), BIT), :] = ref[row : row + BIT, :]

    for plane in range(2):
        put(h_ref, plane * BIT, core, plane, 0)
        put(hx_ref, plane * BIT, 1 - core, plane, 0)
        put(a_ref, plane * BIT, core, plane, 1 + 2 * core)
        put(a_ref, (2 + plane) * BIT, 1 - core, plane, 1 + 2 * core)
        put(ax_ref, plane * BIT, 1 - core, plane, 3 + 2 * core)
        put(ax_ref, (2 + plane) * BIT, core, plane, 3 + 2 * core)
    put(a_ref, 4 * BIT, core, core, 2)
    put(a_ref, 5 * BIT, 1 - core, core, 2)
    put(ax_ref, 4 * BIT, 1 - core, 1 - core, 2)
    put(ax_ref, 5 * BIT, core, 1 - core, 2)
    fresh = []
    for m, w_ref in enumerate((w1_ref, w3_ref, w2_ref)):
        g = jnp.concatenate(
            [all_ref[i * ROWS + m * PART : i * ROWS + (m + 1) * PART, :] for i in range(4)], axis=0
        ).astype(jnp.float32)
        norm = jnp.sqrt(jnp.sum(g * g, keepdims=True)) + 1e-07
        x = (g / norm).astype(jnp.bfloat16)
        for _ in range(NS_STEPS):
            gram = nt(x, x).astype(jnp.bfloat16)
            mixer = (COEF_B * gram.astype(jnp.float32) + COEF_C * nn(gram, gram)).astype(
                jnp.bfloat16
            )
            x = (COEF_A * x.astype(jnp.float32) + nn(mixer, x)).astype(jnp.bfloat16)
        fresh.append((w_ref[...].astype(jnp.float32) - x.astype(jnp.float32)).astype(jnp.bfloat16))
    q = q_ref[...].astype(jnp.float32)
    qn = (q * lax.rsqrt(jnp.mean(q * q, axis=-1, keepdims=True) + EPSILON)).astype(jnp.bfloat16)
    h1 = nt(qn, fresh[0])
    h3 = nt(qn, fresh[1])
    hidden = (h1 * sigmoid(h1) * h3).astype(jnp.bfloat16)
    o = nn(hidden, fresh[2]) * gain_ref[0]
    o_ref[...] = o
    sq_ref[...] = lax.dot_general(
        jnp.ones((8, HD), jnp.float32), o * o, NT,
        precision=lax.Precision.HIGHEST, preferred_element_type=jnp.float32,
    )


def solve(ids, gain, *arrays):
    return pl.pallas_call(
        solve_kernel,
        out_shape=(near_out((TOK, HD), jnp.float32), near_out((8, TOK), jnp.float32)),
        in_specs=[SMEM, SMEM] + [VMEM] * len(arrays),
        out_specs=(VMEM, VMEM),
        scratch_shapes=[pltpu.VMEM((4 * ROWS, HD), jnp.bfloat16)],
        compiler_params=pltpu.CompilerParams(vmem_limit_bytes=28 << 20),
        name="solve",
    )(ids, gain, *[near(x) for x in arrays])


def attend(q, blocks, core, start, foreign):
    places = (
        (TOK, 0),
        (TOK, TOK * (1 - 2 * core)),
        (TOK, -2 * TOK),
        (TOK, -TOK * (1 + 2 * core)),
        (TOK, -4 * TOK),
        (TOK, -TOK * (3 + 2 * core)),
        (FAR, -WINDOW + (FAR - TOK) * core),
        (FAR, -WINDOW + FAR - (FAR + TOK) * core),
    )
    pairs = list(zip(blocks, places))[2 if foreign else 0 :]
    scores = []
    top = None
    for ref, (count, place) in pairs:
        row = lax.broadcasted_iota(jnp.int32, (TOK, count), 0)
        col = lax.broadcasted_iota(jnp.int32, (TOK, count), 1)
        s = nt(q, ref[0:count, :]) * HD ** (-0.5)
        offset = row - col - place
        before = col + (start * TOK + place) < 0
        allowed = (offset >= 0) & (offset < WINDOW)
        allowed = allowed & before if foreign else allowed & jnp.logical_not(before)
        s = jnp.where(allowed, s, -1e30)
        scores.append(s)
        here = jnp.max(s, axis=-1, keepdims=True)
        top = here if top is None else jnp.maximum(top, here)
    if foreign:
        top = top.astype(jnp.bfloat16).astype(jnp.float32)
        weights = [jnp.where(s > -1e29, jnp.exp(s - top), 0.0) for s in scores]
    else:
        weights = [jnp.exp(s - top) for s in scores]
    total = functools.reduce(jnp.add, [jnp.sum(w, axis=-1, keepdims=True) for w in weights])
    inverse = 1.0 / (jnp.maximum(total, 1e-30) if foreign else total)
    o = None
    for w, (ref, (count, _)) in zip(weights, pairs):
        part = nn((w * inverse).astype(jnp.bfloat16), ref[count : 2 * count, :])
        o = part if o is None else o + part
    return o, top, total


def window_kernel(info_ref, q_ref, visitor_ref, *refs):
    blocks = refs[:8]
    o_ref, stat_ref, reply_ref = refs[8:]
    core = info_ref[0]
    start = info_ref[1]
    hosts = info_ref[2] == 1
    o, top, total = attend(q_ref[...], blocks, core, start, False)
    o_ref[...] = o
    stat_ref[...] = in_lanes(jnp.float32, top, total)

    @pl.when(hosts)
    def _():
        o, top, total = attend(visitor_ref[...], blocks, core, start, True)
        high = total.astype(jnp.bfloat16).astype(jnp.float32)
        reply_ref[:, 0:HD] = o.astype(jnp.bfloat16)
        reply_ref[:, HD : HD + 128] = in_lanes(jnp.bfloat16, top, high, total - high)

    @pl.when(jnp.logical_not(hosts))
    def _():
        reply_ref[...] = jnp.zeros_like(reply_ref)


def window_attention(info, *arrays):
    return pl.pallas_call(
        window_kernel,
        out_shape=(
            near_out((TOK, HD), jnp.float32),
            near_out((TOK, 128), jnp.float32),
            near_out((TOK, HD + 128), jnp.bfloat16),
        ),
        in_specs=[SMEM] + [VMEM] * len(arrays),
        out_specs=(VMEM, VMEM, VMEM),
        compiler_params=pltpu.CompilerParams(vmem_limit_bytes=24 << 20),
        name="window",
    )(info, *[near(x) for x in arrays])


def merge_kernel(info_ref, o_ref, stat_ref, reply_ref, out_ref, sq_ref):
    guest = info_ref[3] == 1
    top = stat_ref[:, 0:1]
    total = stat_ref[:, 1:2]
    far_stat = reply_ref[:, HD : HD + 128].astype(jnp.float32)
    far_top = jnp.where(guest, far_stat[:, 0:1], top)
    far_total = jnp.where(guest, far_stat[:, 1:2] + far_stat[:, 2:3], 0.0)
    both = jnp.maximum(top, far_top)
    e1 = total * jnp.exp(top - both)
    e2 = far_total * jnp.exp(far_top - both)
    inverse = 1.0 / (e1 + e2)
    o = o_ref[...] * (e1 * inverse) + reply_ref[:, 0:HD].astype(jnp.float32) * (e2 * inverse)
    out_ref[...] = o
    sq_ref[...] = lax.dot_general(
        jnp.ones((8, HD), jnp.float32), o * o, NT,
        precision=lax.Precision.HIGHEST, preferred_element_type=jnp.float32,
    )


def merge(info, *arrays):
    return pl.pallas_call(
        merge_kernel,
        out_shape=(near_out((TOK, HD), jnp.float32), near_out((8, TOK), jnp.float32)),
        in_specs=[SMEM] + [VMEM] * len(arrays),
        out_specs=(VMEM, VMEM),
        compiler_params=pltpu.CompilerParams(vmem_limit_bytes=8 << 20),
        name="merge",
    )(info, *[near(x) for x in arrays])


def finish_kernel(sums_ref, a_ref, o_ref, wo_ref, fo_ref):
    ones = jnp.ones((HEADS, 128), jnp.float32)
    for which, (src, dst) in enumerate(((a_ref, wo_ref), (o_ref, fo_ref))):
        total = lax.dot_general(
            sums_ref[:, which, :], ones, TN,
            precision=lax.Precision.HIGHEST, preferred_element_type=jnp.float32,
        )[:, 0:1]
        dst[...] = (src[...] * lax.rsqrt(total * (1.0 / (HEADS * HD)) + EPSILON)).astype(
            jnp.bfloat16
        )


def finish(*arrays):
    return pl.pallas_call(
        finish_kernel,
        out_shape=(
            jax.ShapeDtypeStruct((TOK, HD), jnp.bfloat16),
            jax.ShapeDtypeStruct((TOK, HD), jnp.bfloat16),
        ),
        in_specs=[VMEM] * 3,
        out_specs=(VMEM, VMEM),
        compiler_params=pltpu.CompilerParams(vmem_limit_bytes=8 << 20),
        name="finish",
    )(*[near(x) for x in arrays])


def local(queries, key_rows, value_rows, token_rates, fast_one, fast_three, fast_two, head_gain):
    xh = lax.axis_index("xh")
    z = lax.axis_index(RING)
    core = lax.axis_index("core")
    ids = jnp.stack([xh * 2 + core, core, lax.rem(z, 4)]).astype(jnp.int32)
    edge = (z < SPAN).astype(jnp.int32)
    info = jnp.stack([core, z * 2 + core, (1 - xh) * edge, xh * edge]).astype(jnp.int32)

    rate = token_rates[:, 0]
    high = lax.reduce_precision(rate, 8, 7)
    extra = jnp.stack([high, rate - high]).astype(jnp.bfloat16)
    extra = jnp.pad(extra, ((0, 14), (0, HD - TOK)))
    own = jnp.concatenate([key_rows, value_rows, extra], axis=0)

    deep = lax.axis_size(RING)
    own_x = swapped(own, "core")
    across = swapped(own, "xh")
    back1 = forwarded(own)
    w1t = fast_one[0].T
    w3t = fast_three[0].T
    w2 = fast_two[0]
    sofar = gradients(True, ids, own, own_x, w1t, w3t, w2)
    across, sofar = lax.optimization_barrier((across, sofar))
    across_x = swapped(across, "core")
    partial = gradients(False, ids, across, across_x, w1t, w3t, w2, sofar)
    pieces = exchanged(partial.reshape(16, ROWS // 16, HD), SAME)

    visitor = lax.ppermute(queries, CHIPS, [(deep + i, i) for i in range(SPAN)])
    back1_x = swapped(back1, "core")
    back2 = forwarded(back1)
    back2_x = swapped(back2, "core")
    cut = TOK - FAR
    far = jnp.where(
        core == 0,
        jnp.concatenate(
            [back2[FAR:TOK], back2_x[:cut], back2[TOK + FAR : 2 * TOK], back2_x[TOK : TOK + cut]]
        ),
        jnp.concatenate([back2[cut:TOK], back2[TOK + cut : 2 * TOK]]),
    )
    back3 = forwarded(far)
    back3_x = swapped(back3, "core")
    spread = tally(pieces, 8)
    mine = exchanged(spread, KIN).reshape(2 * BIT, HD)
    seen, stats, answer = window_attention(
        info, queries, visitor, own, own_x, back1, back1_x, back2, back2_x, back3, back3_x
    )
    reply = lax.ppermute(answer, CHIPS, [(i, deep + i) for i in range(SPAN)])
    attended, attended_sq = merge(info, seen, stats, reply)

    mine_x = swapped(mine, "core")
    beside = around(jnp.concatenate([mine, mine_x]), 1)
    beyond = around(
        jnp.where(
            core == 0,
            jnp.concatenate([mine[:BIT], mine_x[:BIT]]),
            jnp.concatenate([mine[BIT:], mine_x[BIT:]]),
        ),
        2,
    )
    held = jnp.concatenate([beside, beyond])
    held_x = swapped(held, "core")

    fast, fast_sq = solve(
        ids, head_gain, queries, w1t, w3t, w2, mine, mine_x, held, held_x
    )
    sums = jnp.concatenate([attended_sq[0:1], fast_sq[0:1]], axis=0)
    sums = exchanged(jnp.broadcast_to(sums[None], (HEADS,) + sums.shape), "head")
    return finish(sums, attended, fast)


def solution(mesh):
    fine = Mesh(mesh.devices.reshape(2, 4, 2, 2, 2, 8), CHIPS + ("core", "head"))
    ctx = CHIPS + ("core",)
    return jax.shard_map(
        local,
        mesh=fine,
        in_specs=(
            P(ctx, "head"),
            P(ctx, "head"),
            P(ctx, "head"),
            P(ctx, "head"),
            P("head", None, None),
            P("head", None, None),
            P("head", None, None),
            P("head"),
        ),
        out_specs=(P(ctx, "head"), P(ctx, "head")),
        check_vma=False,
    )
```

```python
import functools

import jax
import jax.numpy as jnp
from jax import lax
from jax.experimental import pallas as pl
from jax.experimental.pallas import tpu as pltpu
from jax.sharding import Mesh
from jax.sharding import PartitionSpec as P

HEADS = 8
HD = 512
FH = 512
WINDOW = 1024
NS_STEPS = 2
TOK = 192
PART = 128
ROWS = 3 * PART

COEF_A = 3.4445
COEF_B = -4.775
COEF_C = 2.0315
EPSILON = 1e-06

BIT = ROWS // 4
FAR = 128
SPAN = 3

CHIPS = ("xh", "zq", "zm", "zl")
RING = ("zq", "zm", "zl")
SAME = ("zm", "zl", "zq")
KIN = ("xh", "zq")

NT = (((1,), (1,)), ((), ()))
TN = (((0,), (0,)), ((), ()))


def swapped(x, axis):
    return lax.ppermute(x, axis, [(0, 1), (1, 0)])


def forwarded(x):
    count = lax.axis_size(RING)
    return lax.ppermute(x, RING, [(i, (i + 1) % count) for i in range(count)])


def around(x, down, up):
    count = lax.axis_size(RING)
    pairs = []
    for i in range(count):
        pairs.append((2 * i, 2 * ((i + down) % count)))
        pairs.append((2 * i + 1, 2 * ((i + up) % count) + 1))
    return lax.ppermute(x, RING + ("core",), pairs)


def exchanged(x, axes):
    return lax.all_to_all(x, axes, 0, 0)


def nt(a, b):
    return lax.dot_general(a, b, NT, preferred_element_type=jnp.float32)


def nn(a, b):
    return jnp.dot(a, b, preferred_element_type=jnp.float32)


def near(x):
    return pltpu.with_memory_space_constraint(x, pltpu.MemorySpace.VMEM)


def distant(x):
    return pltpu.with_memory_space_constraint(x, pltpu.MemorySpace.HBM)


def near_out(shape, dtype):
    return pltpu.MemorySpace.VMEM(shape, dtype)


def sigmoid(x):
    return 1.0 / (1.0 + jnp.exp(-x))


VMEM = pl.BlockSpec(memory_space=pltpu.VMEM)
HBM = pl.BlockSpec(memory_space=pltpu.MemorySpace.HBM)


def in_lanes(dtype, *columns):
    lane = lax.broadcasted_iota(jnp.int32, (TOK, 128), 1)
    out = jnp.zeros((TOK, 128), jnp.float32)
    for i, column in enumerate(columns):
        out = jnp.where(lane == i, column, out)
    return out.astype(dtype)


def pack_kernel(k_ref, v_ref, rate_ref, out_ref, row_ref, sems):
    copies = [
        pltpu.make_async_copy(k_ref, out_ref.at[0:TOK], sems.at[0]),
        pltpu.make_async_copy(v_ref, out_ref.at[TOK : 2 * TOK], sems.at[1]),
        pltpu.make_async_copy(rate_ref, row_ref, sems.at[2]),
    ]
    for copy in copies:
        copy.start()
    copies[2].wait()
    rate = jnp.broadcast_to(row_ref[...], (16, TOK))
    high = rate.astype(jnp.bfloat16).astype(jnp.float32)
    line = lax.broadcasted_iota(jnp.int32, (16, TOK), 0)
    extra = jnp.where(line == 0, high, jnp.where(line == 1, rate - high, 0.0))
    out_ref[2 * TOK : 2 * TOK + 16, :] = jnp.zeros((16, HD), jnp.bfloat16)
    out_ref[2 * TOK : 2 * TOK + 16, 0:TOK] = extra.astype(jnp.bfloat16)
    copies[0].wait()
    copies[1].wait()


def pack(k, v, rate):
    return pl.pallas_call(
        pack_kernel,
        out_shape=near_out((2 * TOK + 16, HD), jnp.bfloat16),
        in_specs=[HBM] * 3,
        out_specs=VMEM,
        scratch_shapes=[pltpu.VMEM((1, TOK), jnp.float32), pltpu.SemaphoreType.DMA((3,))],
        compiler_params=pltpu.CompilerParams(vmem_limit_bytes=4 << 20),
        name="pack",
    )(*[distant(x) for x in (k, v, rate)])


def tally_kernel(pieces_ref, out_ref):
    total = jnp.sum(pieces_ref[...].astype(jnp.float32), axis=0).astype(jnp.bfloat16)
    for i in range(out_ref.shape[0]):
        out_ref[i] = total


def tally(pieces, copies):
    return pl.pallas_call(
        tally_kernel,
        out_shape=jax.ShapeDtypeStruct((copies,) + pieces.shape[1:], jnp.bfloat16),
        in_specs=[VMEM],
        out_specs=VMEM,
        compiler_params=pltpu.CompilerParams(vmem_limit_bytes=4 << 20),
        name="tally",
    )(pieces)


def grad_kernel(first, pa_ref, pb_ref, w1_ref, w3_ref, w2_ref, *rest):
    if first:
        (out_ref,) = rest
    else:
        sofar_ref, out_ref, held_ref, sems = rest
    part = lax.axis_index("xh") * 2 + lax.axis_index("core")
    mine = pl.ds(pl.multiple_of(part * PART, PART), PART)
    w13 = jnp.concatenate([w1_ref[mine, :], w3_ref[mine, :]], axis=0)
    w2 = w2_ref[mine, :]
    ones = jnp.ones((8, HD), jnp.bfloat16)
    g13 = None
    later = []
    for ref in (pa_ref, pb_ref):
        k = ref[0:TOK, :]
        v = ref[TOK : 2 * TOK, :]
        extra = ref[2 * TOK : 2 * TOK + 16, :].astype(jnp.float32)
        rate = -(extra[0:1, 0:TOK] + extra[1:2, 0:TOK])
        kf = k.astype(jnp.float32)
        squares = nt(ones, (kf * kf).astype(jnp.bfloat16))
        scale = lax.rsqrt(squares[0:1, :] * (1.0 / HD) + EPSILON)
        both = nt(w13, k) * scale
        a = both[:PART]
        b = both[PART:]
        s = sigmoid(a)
        u = a * s
        dh = nt(w2, v) * rate
        later.append(((u * b * rate).astype(jnp.bfloat16), v))
        d1 = (dh * b * s * (1.0 + a * (1.0 - s)) * scale).astype(jnp.bfloat16)
        d3 = (dh * u * scale).astype(jnp.bfloat16)
        p13 = nn(jnp.concatenate([d1, d3], axis=0), k)
        g13 = p13 if g13 is None else g13 + p13
    if first:
        out_ref[0 : 2 * PART, :] = g13
        out_ref[2 * PART : ROWS, :] = nn(*later[0]) + nn(*later[1])
        return
    copies = [
        pltpu.make_async_copy(held_ref.at[rows], out_ref.at[rows], sems.at[i])
        for i, rows in enumerate((pl.ds(0, 2 * PART), pl.ds(2 * PART, PART)))
    ]
    held_ref[0 : 2 * PART, :] = (g13 + sofar_ref[0 : 2 * PART, :]).astype(jnp.bfloat16)
    copies[0].start()
    g2 = nn(*later[0]) + nn(*later[1])
    held_ref[2 * PART : ROWS, :] = (g2 + sofar_ref[2 * PART : ROWS, :]).astype(jnp.bfloat16)
    copies[1].start()
    for copy in copies:
        copy.wait()


def gradients(first, *arrays):
    extra = [pltpu.VMEM((ROWS, HD), jnp.bfloat16), pltpu.SemaphoreType.DMA((2,))]
    return pl.pallas_call(
        functools.partial(grad_kernel, first),
        out_shape=near_out((ROWS, HD), jnp.float32)
        if first
        else jax.ShapeDtypeStruct((ROWS, HD), jnp.bfloat16),
        in_specs=[VMEM] * len(arrays),
        out_specs=VMEM if first else HBM,
        scratch_shapes=[] if first else extra,
        compiler_params=pltpu.CompilerParams(vmem_limit_bytes=6 << 20),
        name="grad_first" if first else "grad_second",
    )(*[near(x) for x in arrays])


def solve_kernel(
    q_ref, w1_ref, w3_ref, w2_ref, *refs
):
    blocks = refs[:4]
    scale_ref, o_ref, sq_ref, all_ref, w_ref, query_ref, sems = refs[4:]
    copies = [
        pltpu.make_async_copy(src, dst, sems.at[i])
        for i, (src, dst) in enumerate(
            (
                (w1_ref, w_ref.at[0]),
                (w3_ref, w_ref.at[1]),
                (w2_ref, w_ref.at[2]),
                (q_ref, query_ref),
            )
        )
    ]
    for copy in copies:
        copy.start()
    core = lax.axis_index("core")
    place = lax.rem(lax.axis_index(RING), 4)

    def put(ref, row, which, turn):
        for plane in range(2):
            start = (plane * 2 + which) * ROWS + lax.rem(place + turn, 4) * BIT
            source = row + plane * BIT
            all_ref[pl.ds(pl.multiple_of(start, 32), BIT), :] = ref[source : source + BIT, :]

    for which, (near_ref, far_ref) in ((core, blocks[:2]), (1 - core, blocks[2:])):
        put(near_ref, 0, which, 0)
        for i, turn in enumerate((3, 1, 2)):
            put(far_ref, 2 * i * BIT, which, turn)
    fresh = []
    for m in range(3):
        g = jnp.concatenate(
            [all_ref[i * ROWS + m * PART : i * ROWS + (m + 1) * PART, :] for i in range(4)], axis=0
        ).astype(jnp.float32)
        norm = jnp.sqrt(jnp.sum(g * g, keepdims=True)) + 1e-07
        fresh.append((g * (1.0 / norm)).astype(jnp.bfloat16))
    for _ in range(NS_STEPS):
        grams = [nt(x, x).astype(jnp.bfloat16) for x in fresh]
        mixers = [
            (COEF_B * gram.astype(jnp.float32) + COEF_C * nn(gram, gram)).astype(jnp.bfloat16)
            for gram in grams
        ]
        fresh = [
            (COEF_A * x.astype(jnp.float32) + nn(mixer, x)).astype(jnp.bfloat16)
            for x, mixer in zip(fresh, mixers)
        ]
    for copy in copies:
        copy.wait()
    fresh = [
        (w_ref[m].astype(jnp.float32) - x.astype(jnp.float32)).astype(jnp.bfloat16)
        for m, x in enumerate(fresh)
    ]
    q = query_ref[...].astype(jnp.float32)
    qn = (q * lax.rsqrt(jnp.mean(q * q, axis=-1, keepdims=True) + EPSILON)).astype(jnp.bfloat16)
    h1 = nt(qn, fresh[0])
    h3 = nt(qn, fresh[1])
    hidden = (h1 * sigmoid(h1) * h3).astype(jnp.bfloat16)
    o = nn(hidden, fresh[2]) * scale_ref[...]
    o_ref[...] = o
    sq_ref[...] = lax.dot_general(
        jnp.ones((8, HD), jnp.float32), o * o, NT,
        precision=lax.Precision.HIGHEST, preferred_element_type=jnp.float32,
    )


def solve(outside, inside):
    return pl.pallas_call(
        solve_kernel,
        out_shape=(near_out((TOK, HD), jnp.float32), near_out((8, TOK), jnp.float32)),
        in_specs=[HBM] * len(outside) + [VMEM] * len(inside),
        out_specs=(VMEM, VMEM),
        scratch_shapes=[
            pltpu.VMEM((4 * ROWS, HD), jnp.bfloat16),
            pltpu.VMEM((3, FH, HD), jnp.bfloat16),
            pltpu.VMEM((TOK, HD), jnp.bfloat16),
            pltpu.SemaphoreType.DMA((4,)),
        ],
        compiler_params=pltpu.CompilerParams(vmem_limit_bytes=14 << 20),
        name="solve",
    )(*[distant(x) for x in outside], *[near(x) for x in inside])


def attend(q, blocks, core, start, foreign):
    places = (
        (TOK, 0),
        (TOK, TOK * (1 - 2 * core)),
        (TOK, -2 * TOK),
        (TOK, -TOK * (1 + 2 * core)),
        (TOK, -4 * TOK),
        (TOK, -TOK * (3 + 2 * core)),
        (FAR, -WINDOW + (FAR - TOK) * core),
        (FAR, -WINDOW + FAR - (FAR + TOK) * core),
    )
    pairs = list(zip(blocks, places))[2 if foreign else 0 :]
    scores = []
    top = None
    for ref, (count, place) in pairs:
        row = lax.broadcasted_iota(jnp.int32, (TOK, count), 0)
        col = lax.broadcasted_iota(jnp.int32, (TOK, count), 1)
        s = nt(q, ref[0:count, :]) * HD ** (-0.5)
        offset = row - col - place
        before = col + (start * TOK + place) < 0
        allowed = (offset >= 0) & (offset < WINDOW)
        allowed = allowed & before if foreign else allowed & jnp.logical_not(before)
        s = jnp.where(allowed, s, -1e30)
        scores.append(s)
        here = jnp.max(s, axis=-1, keepdims=True)
        top = here if top is None else jnp.maximum(top, here)
    if foreign:
        top = top.astype(jnp.bfloat16).astype(jnp.float32)
        weights = [jnp.where(s > -1e29, jnp.exp(s - top), 0.0) for s in scores]
    else:
        weights = [jnp.exp(s - top) for s in scores]
    total = functools.reduce(jnp.add, [jnp.sum(w, axis=-1, keepdims=True) for w in weights])
    inverse = 1.0 / (jnp.maximum(total, 1e-30) if foreign else total)
    o = None
    for w, (ref, (count, _)) in zip(weights, pairs):
        part = nn((w * inverse).astype(jnp.bfloat16), ref[count : 2 * count, :])
        o = part if o is None else o + part
    return o, top, total


def window_kernel(q_ref, visitor_ref, *refs):
    blocks = refs[:8]
    o_ref, stat_ref, reply_ref = refs[8:]
    core = lax.axis_index("core")
    z = lax.axis_index(RING)
    start = z * 2 + core
    hosts = (lax.axis_index("xh") == 0) & (z < SPAN)
    o, top, total = attend(q_ref[...], blocks, core, start, False)
    o_ref[...] = o
    stat_ref[...] = in_lanes(jnp.float32, top, total)

    @pl.when(hosts)
    def _():
        o, top, total = attend(visitor_ref[...], blocks, core, start, True)
        high = total.astype(jnp.bfloat16).astype(jnp.float32)
        reply_ref[:, 0:HD] = o.astype(jnp.bfloat16)
        reply_ref[:, HD : HD + 128] = in_lanes(jnp.bfloat16, top, high, total - high)

    @pl.when(jnp.logical_not(hosts))
    def _():
        reply_ref[...] = jnp.zeros_like(reply_ref)


def window_attention(*arrays):
    return pl.pallas_call(
        window_kernel,
        out_shape=(
            near_out((TOK, HD), jnp.float32),
            near_out((TOK, 128), jnp.float32),
            near_out((TOK, HD + 128), jnp.bfloat16),
        ),
        in_specs=[VMEM] * len(arrays),
        out_specs=(VMEM, VMEM, VMEM),
        compiler_params=pltpu.CompilerParams(vmem_limit_bytes=10 << 20),
        name="window",
    )(*[near(x) for x in arrays])


def merge_kernel(o_ref, stat_ref, reply_ref, out_ref, sq_ref):
    guest = (lax.axis_index("xh") == 1) & (lax.axis_index(RING) < SPAN)
    top = stat_ref[:, 0:1]
    total = stat_ref[:, 1:2]
    far_stat = reply_ref[:, HD : HD + 128].astype(jnp.float32)
    far_top = jnp.where(guest, far_stat[:, 0:1], top)
    far_total = jnp.where(guest, far_stat[:, 1:2] + far_stat[:, 2:3], 0.0)
    both = jnp.maximum(top, far_top)
    e1 = total * jnp.exp(top - both)
    e2 = far_total * jnp.exp(far_top - both)
    inverse = 1.0 / (e1 + e2)
    o = o_ref[...] * (e1 * inverse) + reply_ref[:, 0:HD].astype(jnp.float32) * (e2 * inverse)
    out_ref[...] = o
    sq_ref[...] = lax.dot_general(
        jnp.ones((8, HD), jnp.float32), o * o, NT,
        precision=lax.Precision.HIGHEST, preferred_element_type=jnp.float32,
    )


def merge(*arrays):
    return pl.pallas_call(
        merge_kernel,
        out_shape=(near_out((TOK, HD), jnp.float32), near_out((8, TOK), jnp.float32)),
        in_specs=[VMEM] * len(arrays),
        out_specs=(VMEM, VMEM),
        compiler_params=pltpu.CompilerParams(vmem_limit_bytes=4 << 20),
        name="merge",
    )(*[near(x) for x in arrays])


def finish_kernel(sums_ref, a_ref, o_ref, wo_ref, fo_ref):
    ones = jnp.ones((HEADS, 128), jnp.float32)
    for which, (src, dst) in enumerate(((a_ref, wo_ref), (o_ref, fo_ref))):
        total = lax.dot_general(
            sums_ref[:, which, :], ones, TN,
            precision=lax.Precision.HIGHEST, preferred_element_type=jnp.float32,
        )[:, 0:1]
        dst[...] = (src[...] * lax.rsqrt(total * (1.0 / (HEADS * HD)) + EPSILON)).astype(
            jnp.bfloat16
        )


def finish(*arrays):
    return pl.pallas_call(
        finish_kernel,
        out_shape=(
            jax.ShapeDtypeStruct((TOK, HD), jnp.bfloat16),
            jax.ShapeDtypeStruct((TOK, HD), jnp.bfloat16),
        ),
        in_specs=[VMEM] * 3,
        out_specs=(VMEM, VMEM),
        compiler_params=pltpu.CompilerParams(vmem_limit_bytes=4 << 20),
        name="finish",
    )(*[near(x) for x in arrays])


def local(queries, key_rows, value_rows, token_rates, fast_one, fast_three, fast_two, head_gain):
    core = lax.axis_index("core")
    gain = jnp.broadcast_to(head_gain.reshape(1, 1), (1, HD))
    own = pack(key_rows, value_rows, token_rates.T)

    deep = lax.axis_size(RING)
    own_x = swapped(own, "core")
    across = swapped(own, "xh")
    back1 = forwarded(own)
    w1t = fast_one[0].T
    w3t = fast_three[0].T
    w2 = fast_two[0]
    sofar = gradients(True, own, own_x, w1t, w3t, w2)
    across, sofar = lax.optimization_barrier((across, sofar))
    across_x = swapped(across, "core")
    partial = gradients(False, across, across_x, w1t, w3t, w2, sofar)
    pieces = exchanged(partial.reshape(16, ROWS // 16, HD), SAME)

    visitor = lax.ppermute(queries, CHIPS, [(deep + i, i) for i in range(SPAN)])
    back1_x = swapped(back1, "core")
    back2 = forwarded(back1)
    back2_x = swapped(back2, "core")
    cut = TOK - FAR
    far = jnp.where(
        core == 0,
        jnp.concatenate(
            [back2[FAR:TOK], back2_x[:cut], back2[TOK + FAR : 2 * TOK], back2_x[TOK : TOK + cut]]
        ),
        jnp.concatenate([back2[cut:TOK], back2[TOK + cut : 2 * TOK]]),
    )
    back3 = forwarded(far)
    back3_x = swapped(back3, "core")
    spread = tally(pieces, 8)
    mine = exchanged(spread, KIN).reshape(2 * BIT, HD)
    seen, stats, answer = window_attention(
        queries, visitor, own, own_x, back1, back1_x, back2, back2_x, back3, back3_x
    )
    reply = lax.ppermute(answer, CHIPS, [(i, deep + i) for i in range(SPAN)])
    attended, attended_sq = merge(seen, stats, reply)

    above = around(mine, 1, 1)
    below = around(mine, -1, -1)
    beyond = around(mine, -2, 2)
    mine_x = swapped(mine, "core")
    held = jnp.concatenate([above, below, beyond])
    held_x = swapped(held, "core")

    fast, fast_sq = solve(
        (queries, w1t, w3t, w2), (mine, held, mine_x, held_x, gain)
    )
    sums = jnp.concatenate([attended_sq[0:1], fast_sq[0:1]], axis=0)
    sums = exchanged(jnp.broadcast_to(sums[None], (HEADS,) + sums.shape), "head")
    return finish(sums, attended, fast)


def solution(mesh):
    fine = Mesh(mesh.devices.reshape(2, 4, 2, 2, 2, 8), CHIPS + ("core", "head"))
    ctx = CHIPS + ("core",)
    return jax.shard_map(
        local,
        mesh=fine,
        in_specs=(
            P(ctx, "head"),
            P(ctx, "head"),
            P(ctx, "head"),
            P(ctx, "head"),
            P("head", None, None),
            P("head", None, None),
            P("head", None, None),
            P("head"),
        ),
        out_specs=(P(ctx, "head"), P(ctx, "head")),
        check_vma=False,
    )
```

```python
import functools

import jax
import jax.numpy as jnp
from jax import lax
from jax.experimental import pallas as pl
from jax.experimental.pallas import tpu as pltpu
from jax.sharding import Mesh
from jax.sharding import PartitionSpec as P

HEADS = 8
HD = 512
FH = 512
WINDOW = 1024
NS_STEPS = 2
TOK = 192
PART = 128
ROWS = 3 * PART

COEF_A = 3.4445
COEF_B = -4.775
COEF_C = 2.0315
EPSILON = 1e-06

BIT = ROWS // 4
FAR = 128
SPAN = 3

CHIPS = ("xh", "zq", "zm", "zl")
RING = ("zq", "zm", "zl")
SAME = ("zm", "zl", "zq")
KIN = ("xh", "zq")

NT = (((1,), (1,)), ((), ()))
TN = (((0,), (0,)), ((), ()))


def swapped(x, axis):
    return lax.ppermute(x, axis, [(0, 1), (1, 0)])


def forwarded(x):
    count = lax.axis_size(RING)
    return lax.ppermute(x, RING, [(i, (i + 1) % count) for i in range(count)])


def around(x, down, up):
    count = lax.axis_size(RING)
    pairs = []
    for i in range(count):
        pairs.append((2 * i, 2 * ((i + down) % count)))
        pairs.append((2 * i + 1, 2 * ((i + up) % count) + 1))
    return lax.ppermute(x, RING + ("core",), pairs)


def exchanged(x, axes):
    return lax.all_to_all(x, axes, 0, 0)


def nt(a, b):
    return lax.dot_general(a, b, NT, preferred_element_type=jnp.float32)


def nn(a, b):
    return jnp.dot(a, b, preferred_element_type=jnp.float32)


def near(x):
    return pltpu.with_memory_space_constraint(x, pltpu.MemorySpace.VMEM)


def distant(x):
    return pltpu.with_memory_space_constraint(x, pltpu.MemorySpace.HBM)


def near_out(shape, dtype):
    return pltpu.MemorySpace.VMEM(shape, dtype)


def sigmoid(x):
    return 1.0 / (1.0 + jnp.exp(-x))


VMEM = pl.BlockSpec(memory_space=pltpu.VMEM)
HBM = pl.BlockSpec(memory_space=pltpu.MemorySpace.HBM)


def in_lanes(dtype, *columns):
    lane = lax.broadcasted_iota(jnp.int32, (TOK, 128), 1)
    out = jnp.zeros((TOK, 128), jnp.float32)
    for i, column in enumerate(columns):
        out = jnp.where(lane == i, column, out)
    return out.astype(dtype)


def pack_kernel(k_ref, v_ref, rate_ref, out_ref, row_ref, sems):
    copies = [
        pltpu.make_async_copy(k_ref, out_ref.at[0:TOK], sems.at[0]),
        pltpu.make_async_copy(v_ref, out_ref.at[TOK : 2 * TOK], sems.at[1]),
        pltpu.make_async_copy(rate_ref, row_ref, sems.at[2]),
    ]
    for copy in copies:
        copy.start()
    copies[2].wait()
    rate = jnp.broadcast_to(row_ref[...], (16, TOK))
    high = rate.astype(jnp.bfloat16).astype(jnp.float32)
    line = lax.broadcasted_iota(jnp.int32, (16, TOK), 0)
    extra = jnp.where(line == 0, high, jnp.where(line == 1, rate - high, 0.0))
    out_ref[2 * TOK : 2 * TOK + 16, :] = jnp.zeros((16, HD), jnp.bfloat16)
    out_ref[2 * TOK : 2 * TOK + 16, 0:TOK] = extra.astype(jnp.bfloat16)
    copies[0].wait()
    copies[1].wait()


def pack(k, v, rate):
    return pl.pallas_call(
        pack_kernel,
        out_shape=near_out((2 * TOK + 16, HD), jnp.bfloat16),
        in_specs=[HBM] * 3,
        out_specs=VMEM,
        scratch_shapes=[pltpu.VMEM((1, TOK), jnp.float32), pltpu.SemaphoreType.DMA((3,))],
        compiler_params=pltpu.CompilerParams(vmem_limit_bytes=4 << 20),
        name="pack",
    )(*[distant(x) for x in (k, v, rate)])


def tally_kernel(pieces_ref, out_ref):
    total = jnp.sum(pieces_ref[...].astype(jnp.float32), axis=0).astype(jnp.bfloat16)
    for i in range(out_ref.shape[0]):
        out_ref[i] = total


def tally(pieces, copies):
    return pl.pallas_call(
        tally_kernel,
        out_shape=jax.ShapeDtypeStruct((copies,) + pieces.shape[1:], jnp.bfloat16),
        in_specs=[VMEM],
        out_specs=VMEM,
        compiler_params=pltpu.CompilerParams(vmem_limit_bytes=4 << 20),
        name="tally",
    )(pieces)


def grad_kernel(first, pa_ref, pb_ref, w1_ref, w3_ref, w2_ref, *rest):
    if first:
        (out_ref,) = rest
    else:
        sofar_ref, out_ref, held_ref, sems = rest
    part = lax.axis_index("xh") * 2 + lax.axis_index("core")
    mine = pl.ds(pl.multiple_of(part * PART, PART), PART)
    w13 = jnp.concatenate([w1_ref[mine, :], w3_ref[mine, :]], axis=0)
    w2 = w2_ref[mine, :]
    ones = jnp.ones((8, HD), jnp.bfloat16)
    g13 = None
    later = []
    for ref in (pa_ref, pb_ref):
        k = ref[0:TOK, :]
        v = ref[TOK : 2 * TOK, :]
        extra = ref[2 * TOK : 2 * TOK + 16, :].astype(jnp.float32)
        rate = -(extra[0:1, 0:TOK] + extra[1:2, 0:TOK])
        kf = k.astype(jnp.float32)
        squares = nt(ones, (kf * kf).astype(jnp.bfloat16))
        scale = lax.rsqrt(squares[0:1, :] * (1.0 / HD) + EPSILON)
        both = nt(w13, k) * scale
        a = both[:PART]
        b = both[PART:]
        s = sigmoid(a)
        u = a * s
        dh = nt(w2, v) * rate
        later.append(((u * b * rate).astype(jnp.bfloat16), v))
        d1 = (dh * b * s * (1.0 + a * (1.0 - s)) * scale).astype(jnp.bfloat16)
        d3 = (dh * u * scale).astype(jnp.bfloat16)
        p13 = nn(jnp.concatenate([d1, d3], axis=0), k)
        g13 = p13 if g13 is None else g13 + p13
    if first:
        out_ref[0 : 2 * PART, :] = g13
        out_ref[2 * PART : ROWS, :] = nn(*later[0]) + nn(*later[1])
        return
    copies = [
        pltpu.make_async_copy(held_ref.at[rows], out_ref.at[rows], sems.at[i])
        for i, rows in enumerate((pl.ds(0, 2 * PART), pl.ds(2 * PART, PART)))
    ]
    held_ref[0 : 2 * PART, :] = (g13 + sofar_ref[0 : 2 * PART, :]).astype(jnp.bfloat16)
    copies[0].start()
    g2 = nn(*later[0]) + nn(*later[1])
    held_ref[2 * PART : ROWS, :] = (g2 + sofar_ref[2 * PART : ROWS, :]).astype(jnp.bfloat16)
    copies[1].start()
    for copy in copies:
        copy.wait()


def gradients(first, *arrays):
    extra = [pltpu.VMEM((ROWS, HD), jnp.bfloat16), pltpu.SemaphoreType.DMA((2,))]
    return pl.pallas_call(
        functools.partial(grad_kernel, first),
        out_shape=near_out((ROWS, HD), jnp.float32)
        if first
        else jax.ShapeDtypeStruct((ROWS, HD), jnp.bfloat16),
        in_specs=[VMEM] * len(arrays),
        out_specs=VMEM if first else HBM,
        scratch_shapes=[] if first else extra,
        compiler_params=pltpu.CompilerParams(vmem_limit_bytes=6 << 20),
        name="grad_first" if first else "grad_second",
    )(*[near(x) for x in arrays])


def solve_kernel(
    q_ref, w1_ref, w3_ref, w2_ref, *refs
):
    blocks = refs[:4]
    scale_ref, o_ref, sq_ref, all_ref, w_ref, query_ref, sems = refs[4:]
    copies = [
        pltpu.make_async_copy(src, dst, sems.at[i])
        for i, (src, dst) in enumerate(
            (
                (w1_ref, w_ref.at[0]),
                (w3_ref, w_ref.at[1]),
                (w2_ref, w_ref.at[2]),
                (q_ref, query_ref),
            )
        )
    ]
    for copy in copies:
        copy.start()
    core = lax.axis_index("core")
    place = lax.rem(lax.axis_index(RING), 4)

    def put(ref, row, which, turn):
        for plane in range(2):
            start = (plane * 2 + which) * ROWS + lax.rem(place + turn, 4) * BIT
            source = row + plane * BIT
            all_ref[pl.ds(pl.multiple_of(start, 32), BIT), :] = ref[source : source + BIT, :]

    for which, (near_ref, far_ref) in ((core, blocks[:2]), (1 - core, blocks[2:])):
        put(near_ref, 0, which, 0)
        for i, turn in enumerate((1 + 2 * which, 3 + 2 * which, 2)):
            put(far_ref, 2 * i * BIT, which, turn)
    fresh = []
    for m in range(3):
        g = jnp.concatenate(
            [all_ref[i * ROWS + m * PART : i * ROWS + (m + 1) * PART, :] for i in range(4)], axis=0
        ).astype(jnp.float32)
        norm = jnp.sqrt(jnp.sum(g * g, keepdims=True)) + 1e-07
        fresh.append((g * (1.0 / norm)).astype(jnp.bfloat16))
    for _ in range(NS_STEPS):
        grams = [nt(x, x).astype(jnp.bfloat16) for x in fresh]
        mixers = [
            (COEF_B * gram.astype(jnp.float32) + COEF_C * nn(gram, gram)).astype(jnp.bfloat16)
            for gram in grams
        ]
        fresh = [
            (COEF_A * x.astype(jnp.float32) + nn(mixer, x)).astype(jnp.bfloat16)
            for x, mixer in zip(fresh, mixers)
        ]
    for copy in copies:
        copy.wait()
    fresh = [
        (w_ref[m].astype(jnp.float32) - x.astype(jnp.float32)).astype(jnp.bfloat16)
        for m, x in enumerate(fresh)
    ]
    q = query_ref[...].astype(jnp.float32)
    qn = (q * lax.rsqrt(jnp.mean(q * q, axis=-1, keepdims=True) + EPSILON)).astype(jnp.bfloat16)
    h1 = nt(qn, fresh[0])
    h3 = nt(qn, fresh[1])
    hidden = (h1 * sigmoid(h1) * h3).astype(jnp.bfloat16)
    o = nn(hidden, fresh[2]) * scale_ref[...]
    o_ref[...] = o
    sq_ref[...] = lax.dot_general(
        jnp.ones((8, HD), jnp.float32), o * o, NT,
        precision=lax.Precision.HIGHEST, preferred_element_type=jnp.float32,
    )


def solve(outside, inside):
    return pl.pallas_call(
        solve_kernel,
        out_shape=(near_out((TOK, HD), jnp.float32), near_out((8, TOK), jnp.float32)),
        in_specs=[HBM] * len(outside) + [VMEM] * len(inside),
        out_specs=(VMEM, VMEM),
        scratch_shapes=[
            pltpu.VMEM((4 * ROWS, HD), jnp.bfloat16),
            pltpu.VMEM((3, FH, HD), jnp.bfloat16),
            pltpu.VMEM((TOK, HD), jnp.bfloat16),
            pltpu.SemaphoreType.DMA((4,)),
        ],
        compiler_params=pltpu.CompilerParams(vmem_limit_bytes=14 << 20),
        name="solve",
    )(*[distant(x) for x in outside], *[near(x) for x in inside])


def attend(q, blocks, core, start, foreign):
    places = (
        (TOK, 0),
        (TOK, TOK * (1 - 2 * core)),
        (TOK, -2 * TOK),
        (TOK, -TOK * (1 + 2 * core)),
        (TOK, -4 * TOK),
        (TOK, -TOK * (3 + 2 * core)),
        (FAR, -WINDOW + (FAR - TOK) * core),
        (FAR, -WINDOW + FAR - (FAR + TOK) * core),
    )
    pairs = list(zip(blocks, places))[2 if foreign else 0 :]
    scores = []
    top = None
    for ref, (count, place) in pairs:
        row = lax.broadcasted_iota(jnp.int32, (TOK, count), 0)
        col = lax.broadcasted_iota(jnp.int32, (TOK, count), 1)
        s = nt(q, ref[0:count, :]) * HD ** (-0.5)
        offset = row - col - place
        before = col + (start * TOK + place) < 0
        allowed = (offset >= 0) & (offset < WINDOW)
        allowed = allowed & before if foreign else allowed & jnp.logical_not(before)
        s = jnp.where(allowed, s, -1e30)
        scores.append(s)
        here = jnp.max(s, axis=-1, keepdims=True)
        top = here if top is None else jnp.maximum(top, here)
    if foreign:
        top = top.astype(jnp.bfloat16).astype(jnp.float32)
        weights = [jnp.where(s > -1e29, jnp.exp(s - top), 0.0) for s in scores]
    else:
        weights = [jnp.exp(s - top) for s in scores]
    total = functools.reduce(jnp.add, [jnp.sum(w, axis=-1, keepdims=True) for w in weights])
    inverse = 1.0 / (jnp.maximum(total, 1e-30) if foreign else total)
    o = None
    for w, (ref, (count, _)) in zip(weights, pairs):
        part = nn((w * inverse).astype(jnp.bfloat16), ref[count : 2 * count, :])
        o = part if o is None else o + part
    return o, top, total


def window_kernel(q_ref, visitor_ref, *refs):
    blocks = refs[:8]
    o_ref, stat_ref, reply_ref = refs[8:]
    core = lax.axis_index("core")
    z = lax.axis_index(RING)
    start = z * 2 + core
    hosts = (lax.axis_index("xh") == 0) & (z < SPAN)
    o, top, total = attend(q_ref[...], blocks, core, start, False)
    o_ref[...] = o
    stat_ref[...] = in_lanes(jnp.float32, top, total)

    @pl.when(hosts)
    def _():
        o, top, total = attend(visitor_ref[...], blocks, core, start, True)
        high = total.astype(jnp.bfloat16).astype(jnp.float32)
        reply_ref[:, 0:HD] = o.astype(jnp.bfloat16)
        reply_ref[:, HD : HD + 128] = in_lanes(jnp.bfloat16, top, high, total - high)

    @pl.when(jnp.logical_not(hosts))
    def _():
        reply_ref[...] = jnp.zeros_like(reply_ref)


def window_attention(*arrays):
    return pl.pallas_call(
        window_kernel,
        out_shape=(
            near_out((TOK, HD), jnp.float32),
            near_out((TOK, 128), jnp.float32),
            near_out((TOK, HD + 128), jnp.bfloat16),
        ),
        in_specs=[VMEM] * len(arrays),
        out_specs=(VMEM, VMEM, VMEM),
        compiler_params=pltpu.CompilerParams(vmem_limit_bytes=10 << 20),
        name="window",
    )(*[near(x) for x in arrays])


def merge_kernel(o_ref, stat_ref, reply_ref, out_ref, sq_ref):
    guest = (lax.axis_index("xh") == 1) & (lax.axis_index(RING) < SPAN)
    top = stat_ref[:, 0:1]
    total = stat_ref[:, 1:2]
    far_stat = reply_ref[:, HD : HD + 128].astype(jnp.float32)
    far_top = jnp.where(guest, far_stat[:, 0:1], top)
    far_total = jnp.where(guest, far_stat[:, 1:2] + far_stat[:, 2:3], 0.0)
    both = jnp.maximum(top, far_top)
    e1 = total * jnp.exp(top - both)
    e2 = far_total * jnp.exp(far_top - both)
    inverse = 1.0 / (e1 + e2)
    o = o_ref[...] * (e1 * inverse) + reply_ref[:, 0:HD].astype(jnp.float32) * (e2 * inverse)
    out_ref[...] = o
    sq_ref[...] = lax.dot_general(
        jnp.ones((8, HD), jnp.float32), o * o, NT,
        precision=lax.Precision.HIGHEST, preferred_element_type=jnp.float32,
    )


def merge(*arrays):
    return pl.pallas_call(
        merge_kernel,
        out_shape=(near_out((TOK, HD), jnp.float32), near_out((8, TOK), jnp.float32)),
        in_specs=[VMEM] * len(arrays),
        out_specs=(VMEM, VMEM),
        compiler_params=pltpu.CompilerParams(vmem_limit_bytes=4 << 20),
        name="merge",
    )(*[near(x) for x in arrays])


def finish_kernel(sums_ref, a_ref, o_ref, wo_ref, fo_ref):
    ones = jnp.ones((HEADS, 128), jnp.float32)
    for which, (src, dst) in enumerate(((a_ref, wo_ref), (o_ref, fo_ref))):
        total = lax.dot_general(
            sums_ref[:, which, :], ones, TN,
            precision=lax.Precision.HIGHEST, preferred_element_type=jnp.float32,
        )[:, 0:1]
        dst[...] = (src[...] * lax.rsqrt(total * (1.0 / (HEADS * HD)) + EPSILON)).astype(
            jnp.bfloat16
        )


def finish(*arrays):
    return pl.pallas_call(
        finish_kernel,
        out_shape=(
            jax.ShapeDtypeStruct((TOK, HD), jnp.bfloat16),
            jax.ShapeDtypeStruct((TOK, HD), jnp.bfloat16),
        ),
        in_specs=[VMEM] * 3,
        out_specs=(VMEM, VMEM),
        compiler_params=pltpu.CompilerParams(vmem_limit_bytes=4 << 20),
        name="finish",
    )(*[near(x) for x in arrays])


def local(queries, key_rows, value_rows, token_rates, fast_one, fast_three, fast_two, head_gain):
    core = lax.axis_index("core")
    gain = jnp.broadcast_to(head_gain.reshape(1, 1), (1, HD))
    own = pack(key_rows, value_rows, token_rates.T)

    deep = lax.axis_size(RING)
    own_x = swapped(own, "core")
    across = swapped(own, "xh")
    back1 = forwarded(own)
    w1t = fast_one[0].T
    w3t = fast_three[0].T
    w2 = fast_two[0]
    sofar = gradients(True, own, own_x, w1t, w3t, w2)
    across, sofar = lax.optimization_barrier((across, sofar))
    across_x = swapped(across, "core")
    partial = gradients(False, across, across_x, w1t, w3t, w2, sofar)
    pieces = exchanged(partial.reshape(16, ROWS // 16, HD), SAME)

    visitor = lax.ppermute(queries, CHIPS, [(deep + i, i) for i in range(SPAN)])
    back1_x = swapped(back1, "core")
    back2 = forwarded(back1)
    back2_x = swapped(back2, "core")
    cut = TOK - FAR
    far = jnp.where(
        core == 0,
        jnp.concatenate(
            [back2[FAR:TOK], back2_x[:cut], back2[TOK + FAR : 2 * TOK], back2_x[TOK : TOK + cut]]
        ),
        jnp.concatenate([back2[cut:TOK], back2[TOK + cut : 2 * TOK]]),
    )
    back3 = forwarded(far)
    back3_x = swapped(back3, "core")
    spread = tally(pieces, 8)
    mine = exchanged(spread, KIN).reshape(2 * BIT, HD)
    seen, stats, answer = window_attention(
        queries, visitor, own, own_x, back1, back1_x, back2, back2_x, back3, back3_x
    )
    reply = lax.ppermute(answer, CHIPS, [(i, deep + i) for i in range(SPAN)])
    attended, attended_sq = merge(seen, stats, reply)

    above = around(mine, -1, 1)
    below = around(mine, 1, -1)
    beyond = around(mine, -2, 2)
    mine_x = swapped(mine, "core")
    held = jnp.concatenate([above, below, beyond])
    held_x = swapped(held, "core")

    fast, fast_sq = solve(
        (queries, w1t, w3t, w2), (mine, held, mine_x, held_x, gain)
    )
    sums = jnp.concatenate([attended_sq[0:1], fast_sq[0:1]], axis=0)
    sums = exchanged(jnp.broadcast_to(sums[None], (HEADS,) + sums.shape), "head")
    return finish(sums, attended, fast)


def solution(mesh):
    fine = Mesh(mesh.devices.reshape(2, 4, 2, 2, 2, 8), CHIPS + ("core", "head"))
    ctx = CHIPS + ("core",)
    return jax.shard_map(
        local,
        mesh=fine,
        in_specs=(
            P(ctx, "head"),
            P(ctx, "head"),
            P(ctx, "head"),
            P(ctx, "head"),
            P("head", None, None),
            P("head", None, None),
            P("head", None, None),
            P("head"),
        ),
        out_specs=(P(ctx, "head"), P(ctx, "head")),
        check_vma=False,
    )
```
